256 devices in a mesh: dp: 16 (over x, y), head: 16 (over z, core).
Axes of the slice: x: 4, y: 4, z: 8, core: 2. Of those that a mesh axis runs over, the one named last changes fastest.
Arguments:
- query: bfloat16 [32768, 12288], P(('dp', 'head')), may hold values from -160 to 160
- latent: bfloat16 [32768, 576], P(('dp', 'head')), may hold values from -6 to 6
- d_attn: bfloat16 [32768, 8192], P(('dp', 'head')), may hold values from -6 to 6
- w_kv: bfloat16 [512, 16384], P('dp', 'head'), may hold values from -0.25 to 0.25
- doc_lengths: int32 [16, 10], P('dp'), may hold values from 1 to 384, 2048 in all within a row
Outputs:
- d_query: bfloat16 [32768, 12288], P(('dp', 'head'))
- d_latent: float32 [32768, 576], P(('dp', 'head'))
- d_w_kv: float32 [512, 16384], P('dp', 'head')
The draws below stay inside these ranges and needn't reach their ends.
Inputs may be any that keep to these rules, and one draw needn't show every extreme that they name: `doc_lengths`: row g lists the lengths of the 10 documents of data group g; they sum to 2048, and the longest of each row is exactly 384.
All inputs are finite; a program needn't handle non-finite values.
Results may differ from the reference program's by a relative error of at most 0.025.
Values may be sent and summed in bfloat16 or wider, within the bound.
No kernel may reach another device: no remote copies, remote signals or barrier semaphores. Data moves between devices by JAX's collectives and lax.ppermute only.
A program may use at most 128 MiB of HBM per device.

```python
import math
import jax
import jax.numpy as jnp
import numpy as np
from jax import lax

HEADS = 64
NOPE = 128
ROPE = 64
VDIM = 128
KV_RANK = 512
DOC_MAX = 384
QB = 128
SEQ = 2048
GROUPS = 16
TOKENS = 32768
NDOC = 10


def joint_tables(key):
    base = jax.random.fold_in(key, 4242)
    keys_list = jax.random.split(base, 2)
    latent = jnp.clip(jax.random.normal(keys_list[0], (TOKENS, KV_RANK + ROPE), jnp.float32), -6.0, 6.0)
    query = jnp.clip(jax.random.normal(keys_list[1], (TOKENS, HEADS * (NOPE + ROPE)), jnp.float32), -6.0, 6.0)
    return (query, latent)


def draw_query(key, part):
    return joint_tables(key)[0].astype(jnp.bfloat16)


def draw_latent(key, part):
    return joint_tables(key)[1].astype(jnp.bfloat16)


def steps_of(key, dims, pieces, low, top_value):
    level = 1.0
    for dim, shards_of in pieces:
        heights = jax.random.uniform(jax.random.fold_in(jax.random.fold_in(key, 6), dim), (shards_of,), jnp.float32, low / len(pieces), top_value / len(pieces))
        level = level * jnp.repeat(jnp.exp(heights), dims[dim] // shards_of).reshape((-1,) + (1,) * (len(dims) - 1 - dim))
    return level


def split_up(count, total, limit, skew):
    weights = [(1 << 20) // math.isqrt(standing ** skew) + 1 for standing in range(2, count + 1)]
    rest, holding = total - limit - (count - 1), [1] * (count - 1)
    while rest > 0:
        candidates = [i for i in range(count - 1) if holding[i] < limit]
        pool, budget = sum([weights[i] for i in candidates]), rest
        for i in candidates:
            addition = min(limit - holding[i], max(1, budget * weights[i] // pool), rest)
            holding[i] = holding[i] + addition
            rest = rest - addition
    return np.array([limit] + holding)


def ragged_sizes(stream_key, number_of, total, most, slope):
    if number_of == 2:
        one = jax.random.randint(stream_key, (), max(1, total - most), min(most, total - 1) + 1)
        return jnp.stack([one, total - one])
    sizes = jnp.asarray(split_up(number_of, total, most, slope), jnp.int32)
    couples = (number_of - 1) // 2
    source_of, sink = sizes[1:1 + 2 * couples:2], sizes[2:2 + 2 * couples:2]
    room = jnp.minimum(source_of - 1, most - sink)
    shifted = jax.random.randint(jax.random.fold_in(stream_key, 1), (couples,), 0, 1 << 20) % (room + 1)
    sizes = sizes.at[1:1 + 2 * couples:2].set(source_of - shifted).at[2:2 + 2 * couples:2].set(sink + shifted)
    return sizes[jax.random.permutation(jax.random.fold_in(stream_key, 2), number_of)]


def normal_values(key, extent, spread, limit, cuts=(), held_as=jnp.bfloat16):
    values = jax.random.normal(key, extent, jnp.float32) * spread
    if len(cuts) > 0:
        values = steps_of(key, extent, cuts, -0.22, 0.18) * values
    return jnp.clip(values, min=-limit, max=limit).astype(held_as)


def setup_inputs(seed: int = 0) -> dict:
    seeds = jax.random.split(jax.random.key(seed), 6)
    return {
        "query": draw_query(jax.random.fold_in(seeds[5], 71), 0),
        "latent": draw_latent(jax.random.fold_in(seeds[5], 71), 0),
        "d_attn": normal_values(seeds[2], (TOKENS, HEADS * VDIM), 1.0, 6.0, ((0, 256),)),
        "w_kv": normal_values(seeds[3], (KV_RANK, HEADS * (NOPE + VDIM)), KV_RANK ** -0.5, 0.25, ((0, 16), (1, 16))),
        "doc_lengths": jax.vmap(lambda own: ragged_sizes(own, NDOC, SEQ, DOC_MAX, 1))(jax.random.split(seeds[4], GROUPS)).reshape((GROUPS, NDOC)).astype(jnp.int32),
    }


masked_score = -1e+30

def document_index(lengths_row, count):
    ends = jnp.cumsum(lengths_row).astype(jnp.int32)
    positions = jnp.arange(count, dtype=jnp.int32)
    return lax.optimization_barrier(jnp.sum((positions[:, None] >= ends[None, :]).astype(jnp.int32), axis=1)).astype(jnp.int32)

def attend_backward(queries, keys_padded, values_padded, grads_out, doc_padded, block, window):
    seq_len = queries.shape[0]
    reach = window - block
    scale = 1.0 / math.sqrt(queries.shape[2])
    blocks = seq_len // block

    def one_block(carry, index):
        grad_keys, grad_values = carry
        first = index * block
        query_rows = lax.dynamic_slice_in_dim(queries, first, block, 0).astype(jnp.float32)
        key_rows = lax.dynamic_slice_in_dim(keys_padded, first, window, 0).astype(jnp.float32)
        value_rows = lax.dynamic_slice_in_dim(values_padded, first, window, 0).astype(jnp.float32)
        out_rows = lax.dynamic_slice_in_dim(grads_out, first, block, 0).astype(jnp.float32)
        query_doc = lax.dynamic_slice_in_dim(doc_padded, first + reach, block, 0)
        key_doc = lax.dynamic_slice_in_dim(doc_padded, first, window, 0)
        query_pos = jnp.arange(block, dtype=jnp.int32) + reach
        key_pos = jnp.arange(window, dtype=jnp.int32)
        allowed = (key_pos[None, :] <= query_pos[:, None]) & (key_doc[None, :] == query_doc[:, None])
        scores = jnp.einsum('qhd,khd->hqk', query_rows, key_rows) * scale
        scores = jnp.where(allowed[None], scores, masked_score)
        top = lax.optimization_barrier(jnp.max(scores, axis=2, keepdims=True))
        weights = jnp.exp(scores - top)
        probs = weights / lax.optimization_barrier(jnp.sum(weights, axis=2, keepdims=True))
        probs_low = probs.astype(jnp.bfloat16).astype(jnp.float32)
        attn_out = jnp.einsum('hqk,khd->qhd', probs_low, value_rows)
        delta = lax.optimization_barrier(jnp.sum(out_rows * attn_out, axis=2))
        dprob = jnp.einsum('qhd,khd->hqk', out_rows, value_rows)
        dscore = probs * (dprob - jnp.transpose(delta)[:, :, None])
        dscore_low = dscore.astype(jnp.bfloat16).astype(jnp.float32)
        grad_query = jnp.einsum('hqk,khd->qhd', dscore_low, key_rows) * scale
        grad_key_rows = jnp.einsum('hqk,qhd->khd', dscore_low, query_rows) * scale
        grad_value_rows = jnp.einsum('hqk,qhd->khd', probs_low, out_rows)
        grad_keys = lax.dynamic_update_slice_in_dim(grad_keys, lax.dynamic_slice_in_dim(grad_keys, first, window, 0) + grad_key_rows, first, 0)
        grad_values = lax.dynamic_update_slice_in_dim(grad_values, lax.dynamic_slice_in_dim(grad_values, first, window, 0) + grad_value_rows, first, 0)
        return ((grad_keys, grad_values), grad_query.astype(jnp.bfloat16))
    start_keys = jnp.zeros(keys_padded.shape, jnp.float32)
    start_values = jnp.zeros(values_padded.shape, jnp.float32)
    (grad_keys, grad_values), grad_queries = lax.scan(one_block, (start_keys, start_values), jnp.arange(blocks, dtype=jnp.int32))
    grad_queries = grad_queries.reshape(seq_len, queries.shape[1], queries.shape[2])
    return (grad_keys[reach:], grad_values[reach:], grad_queries)

def group_backward(query_g, latent_g, grads_g, w_kv, lengths_row):
    seq_len = query_g.shape[0]
    compressed = latent_g[:, :KV_RANK]
    kv_up = jnp.dot(compressed, w_kv, preferred_element_type=jnp.float32).astype(jnp.bfloat16)
    kv_up = kv_up.reshape(seq_len, HEADS, NOPE + VDIM)
    rotary = jnp.broadcast_to(latent_g[:, None, KV_RANK:], (seq_len, HEADS, ROPE))
    keys = jnp.concatenate([kv_up[:, :, :NOPE], rotary], axis=2)
    values = kv_up[:, :, NOPE:]
    keys_padded = jnp.concatenate([jnp.zeros((DOC_MAX, HEADS, NOPE + ROPE), keys.dtype), keys], axis=0)
    values_padded = jnp.concatenate([jnp.zeros((DOC_MAX, HEADS, VDIM), values.dtype), values], axis=0)
    doc_ids = document_index(lengths_row, seq_len)
    doc_padded = jnp.concatenate([jnp.full((DOC_MAX,), -1, jnp.int32), doc_ids]).astype(jnp.int32)
    grad_keys, grad_values, grad_queries = attend_backward(query_g.reshape(seq_len, HEADS, NOPE + ROPE), keys_padded, values_padded, grads_g.reshape(seq_len, HEADS, VDIM), doc_padded, QB, DOC_MAX + QB)
    grad_kv = jnp.concatenate([grad_keys[:, :, :NOPE], grad_values], axis=2).astype(jnp.bfloat16)
    grad_kv = grad_kv.reshape(seq_len, HEADS * (NOPE + VDIM))
    grad_weight = jnp.dot(jnp.transpose(compressed), grad_kv, preferred_element_type=jnp.float32)
    grad_compressed = jnp.dot(grad_kv, jnp.transpose(w_kv), preferred_element_type=jnp.float32)
    grad_rotary = lax.optimization_barrier(jnp.sum(grad_keys[:, :, NOPE:], axis=1))
    grad_latent = jnp.concatenate([grad_compressed, grad_rotary], axis=1)
    return (grad_queries.reshape(seq_len, HEADS * (NOPE + ROPE)), grad_latent, grad_weight)

def reference(query, latent, d_attn, w_kv, doc_lengths):

    def one_group(carry, index):
        first = index * SEQ
        query_g = lax.dynamic_slice_in_dim(query, first, SEQ, 0)
        latent_g = lax.dynamic_slice_in_dim(latent, first, SEQ, 0)
        grads_g = lax.dynamic_slice_in_dim(d_attn, first, SEQ, 0)
        lengths_row = lax.dynamic_index_in_dim(doc_lengths, index, 0, keepdims=False)
        grad_q, grad_l, grad_w = group_backward(query_g, latent_g, grads_g, w_kv, lengths_row)
        return (carry + grad_w, (grad_q, grad_l))
    start_weight = jnp.zeros((KV_RANK, HEADS * (NOPE + VDIM)), jnp.float32)
    total_weight, (all_q, all_l) = lax.scan(one_group, start_weight, jnp.arange(GROUPS, dtype=jnp.int32))
    d_query = all_q.reshape(TOKENS, HEADS * (NOPE + ROPE))
    d_latent = all_l.reshape(TOKENS, KV_RANK + ROPE)
    return (d_query, d_latent, total_weight)
```

```python
import functools
import math

import jax
import jax.numpy as jnp
from jax import lax
from jax.experimental import pallas as pl
from jax.experimental.pallas import tpu as pltpu
from jax.sharding import Mesh, PartitionSpec as P


NOPE = 128
ROPE = 64
VDIM = 128
QK = NOPE + ROPE
KV_RANK = 512
NX, NY, NZ, NC = 4, 4, 8, 2
BLOCK = 128
CHIP = NC * BLOCK
WINDOW = 5 * BLOCK
HALF = NZ // 2
ROWS = KV_RANK // (NX * NY)
BAND = 4 * ROWS
PAIR = 2 * (NOPE + VDIM)
SCALE = 1.0 / math.sqrt(QK)
MASKED = -1e30


F32 = jnp.float32
BF16 = jnp.bfloat16
SIZES = {"x": NX, "y": NY, "z": NZ, "core": NC}
NT = (((1,), (1,)), ((), ()))
TN = (((0,), (0,)), ((), ()))


def shift(value, axis, step):
    size = SIZES[axis]
    return lax.ppermute(value, axis, [(i, (i + step) % size) for i in range(size)])


def shifts(value, axis):
    return [value] + [shift(value, axis, s) for s in range(1, SIZES[axis])]


def scatter_shifts(pieces, axis):
    return [pieces[0]] + [shift(pieces[s], axis, s) for s in range(1, SIZES[axis])]


def around(position, step, size):
    return lax.rem(position + (step % size), size)


def whole(kernel, scalars, arrays, out_shapes):
    specs = pl.BlockSpec(memory_space=pltpu.VMEM)
    moved = sum(a.size * a.dtype.itemsize for a in arrays)
    moved += sum(math.prod(o.shape) * o.dtype.itemsize for o in out_shapes)
    return pl.pallas_call(
        kernel,
        out_shape=out_shapes,
        in_specs=[pl.BlockSpec(memory_space=pltpu.SMEM)] + [specs] * len(arrays),
        out_specs=[specs] * len(out_shapes),
        cost_estimate=pl.CostEstimate(flops=0, bytes_accessed=moved, transcendentals=0),
    )(scalars, *arrays)


def pack_kernel(sc, q_ref, g_ref, q_out, g_out):
    q_out[...] = q_ref[...]
    g_out[...] = g_ref[...]


def pack_other(core, query, d_attn):
    qw, gw = query.shape[1] // 16, d_attn.shape[1] // 16
    return pl.pallas_call(
        pack_kernel,
        out_shape=[
            jax.ShapeDtypeStruct((BLOCK, 8 * qw), BF16),
            jax.ShapeDtypeStruct((BLOCK, 8 * gw), BF16),
        ],
        grid_spec=pltpu.PrefetchScalarGridSpec(
            num_scalar_prefetch=1,
            grid=(8,),
            in_specs=[
                pl.BlockSpec((BLOCK, qw), lambda k, sc: (0, 2 * k + 1 - sc[0])),
                pl.BlockSpec((BLOCK, gw), lambda k, sc: (0, 2 * k + 1 - sc[0])),
            ],
            out_specs=[
                pl.BlockSpec((BLOCK, qw), lambda k, sc: (0, k)),
                pl.BlockSpec((BLOCK, gw), lambda k, sc: (0, k)),
            ],
        ),
        cost_estimate=pl.CostEstimate(
            flops=0, bytes_accessed=BLOCK * 16 * (qw + gw) * 2, transcendentals=0
        ),
    )(core, query, d_attn)


Z_STEPS = (0, 1, -1, 2)


def z_assemble(z, pieces):
    def kernel(sc, *refs):
        ins, (x_out, y_out) = refs[:4], refs[4:]
        for s, ref in zip(Z_STEPS, ins):
            for far in range(2):
                at = around(sc[0], -s - HALF * far, NZ)
                x_out[at] = ref[far, :, :PAIR]
                y_out[at] = ref[far, :, PAIR:]

    shape = jax.ShapeDtypeStruct((NZ, ROWS, PAIR), BF16)
    return whole(kernel, z, pieces, [shape, shape])


def mid_assemble(position, pieces):
    def kernel(sc, *refs):
        ins, outs = refs[:4], refs[4:]
        for s in range(4):
            at = pl.ds(pl.multiple_of(around(sc[0], -s, 4) * ROWS, ROWS), ROWS)
            for half in range(2):
                outs[half][:, at, :] = ins[s][half * HALF : (half + 1) * HALF]

    shape = jax.ShapeDtypeStruct((HALF, BAND, PAIR), BF16)
    return whole(kernel, position, pieces, [shape, shape])


def first_reduce(position, pieces0, pieces1):
    def kernel(sc, *refs):
        outs = refs[8:]
        for half in range(2):
            ins = refs[4 * half : 4 * half + 4]
            for s in range(4):
                at = pl.ds(pl.multiple_of(around(sc[0], s, 4) * ROWS, ROWS), ROWS)
                total = ins[0][:, at, :].astype(F32)
                for ref in ins[1:]:
                    total = total + ref[:, at, :].astype(F32)
                outs[s][half * HALF : (half + 1) * HALF] = total.astype(BF16)

    shape = jax.ShapeDtypeStruct((NZ, ROWS, PAIR), BF16)
    return whole(kernel, position, list(pieces0) + list(pieces1), [shape] * 4)


def second_reduce(z, x_pieces, y_pieces):
    def kernel(sc, *refs):
        outs = refs[8:]
        for s, out in zip(Z_STEPS, outs):
            for far in range(2):
                at = around(sc[0], s + HALF * far, NZ)
                for color in range(2):
                    ins = refs[4 * color : 4 * color + 4]
                    total = ins[0][at].astype(F32)
                    for ref in ins[1:]:
                        total = total + ref[at].astype(F32)
                    out[far, :, color * PAIR : (color + 1) * PAIR] = total.astype(BF16)

    shape = jax.ShapeDtypeStruct((2, ROWS, 2 * PAIR), BF16)
    return whole(kernel, z, list(x_pieces) + list(y_pieces), [shape] * 4)


def third_reduce(z, pieces):
    def kernel(sc, *refs):
        for far in range(2):
            total = refs[0][far].astype(F32)
            for ref in refs[1:4]:
                total = total + ref[far].astype(F32)
            refs[4 + far][...] = total.astype(refs[4 + far].dtype)

    shape = (ROWS, 2 * PAIR)
    return whole(
        kernel, z, pieces, [jax.ShapeDtypeStruct(shape, F32), jax.ShapeDtypeStruct(shape, BF16)]
    )


def band_copies(color, position, step):
    index = around(position, step, 4)
    if color == 0:
        yield pl.ds(pl.multiple_of(index * BAND, BAND), BAND), slice(0, BAND)
    else:
        for x in range(NX):
            start = pl.multiple_of(index * ROWS + x * BAND, ROWS)
            yield pl.ds(start, ROWS), slice(x * ROWS, (x + 1) * ROWS)


def attend_kernel(color, first, sc, *refs):
    lat, lat_t, rope, bias, q_own, q_oth, g_own, g_oth = refs[:8]
    weights = refs[8:12]
    refs = refs[12:]
    if not first:
        sum_in, rope_in, _ = refs[:3]
        refs = refs[3:]
    dq_own, dq_oth = refs[:2]
    d_weights = refs[2:6]
    d_lat, d_rope = refs[6:8]
    w_buf, q_buf, g_buf, dq_buf, dkv_buf, dw_buf = refs[8:]
    core, position = sc[0], sc[1 + color]

    @pl.when(pl.program_id(0) == 0)
    def _():
        if first:
            d_lat[...] = jnp.zeros_like(d_lat)
            d_rope[...] = jnp.zeros_like(d_rope)
        else:
            d_lat[...] = sum_in[...]
            d_rope[...] = rope_in[...]

    for s in range(4):
        for there, here in band_copies(color, position, -s):
            w_buf[there, :] = weights[s][0, here, :]
    own = pl.ds(pl.multiple_of(core * BLOCK, BLOCK), BLOCK)
    oth = pl.ds(pl.multiple_of((1 - core) * BLOCK, BLOCK), BLOCK)
    q_buf[own, :] = q_own[...]
    q_buf[oth, :] = q_oth[...]
    g_buf[own, :] = g_own[...]
    g_buf[oth, :] = g_oth[...]

    kv = jnp.dot(lat[...], w_buf[...], preferred_element_type=F32).astype(BF16)
    for h in range(2):
        base = h * (NOPE + VDIM)
        key = jnp.concatenate([kv[:, base : base + NOPE], rope[...]], axis=1)
        value = kv[:, base + NOPE : base + NOPE + VDIM]
        q = q_buf[:, h * QK : (h + 1) * QK]
        g = g_buf[:, h * VDIM : (h + 1) * VDIM]
        scores = lax.dot_general(key, q, NT, preferred_element_type=F32)
        scores = scores * (SCALE * math.log2(math.e)) + bias[...]
        top = jnp.max(scores, axis=0, keepdims=True)
        expd = jnp.exp2(scores - top)
        probs = expd * (1.0 / jnp.sum(expd, axis=0, keepdims=True))
        probs_low = probs.astype(BF16)
        d_prob = lax.dot_general(value, g, NT, preferred_element_type=F32)
        delta = jnp.sum(probs_low.astype(F32) * d_prob, axis=0, keepdims=True)
        d_score = (probs * (d_prob - delta)).astype(BF16)
        d_q = lax.dot_general(d_score, key, TN, preferred_element_type=F32) * SCALE
        d_key = jnp.dot(d_score, q, preferred_element_type=F32) * SCALE
        d_value = jnp.dot(probs_low, g, preferred_element_type=F32)
        dq_buf[:, h * QK : (h + 1) * QK] = d_q.astype(BF16)
        dkv_buf[:, base : base + NOPE] = d_key[:, :NOPE].astype(BF16)
        dkv_buf[:, base + NOPE : base + NOPE + VDIM] = d_value.astype(BF16)
        d_rope[...] += d_key[:, NOPE:]

    dq_own[...] = dq_buf[own, :]
    dq_oth[...] = dq_buf[oth, :]
    dw_buf[...] = jnp.dot(lat_t[...], dkv_buf[...], preferred_element_type=F32).astype(BF16)
    for s in range(4):
        for there, here in band_copies(color, position, s):
            d_weights[s][0, here, :] = dw_buf[there, :]
    d_lat[...] += lax.dot_general(dkv_buf[...], w_buf[...], NT, preferred_element_type=F32)


def attend(color, half, scalars, window, query, q_oth, d_attn, g_oth, weights, carried):
    first = carried is None
    resident = pl.BlockSpec(memory_space=pltpu.VMEM)
    qw, gw = 2 * QK, 2 * VDIM

    def own_block(k, sc):
        return (0, 4 * (k + half * HALF) + 2 * sc[0] + color)

    def oth_block(k, sc):
        return (0, 2 * (k + half * HALF) + color)

    piece = pl.BlockSpec((1, BAND, PAIR), lambda k, sc: (k, 0, 0))
    in_specs = [resident] * 4 + [
        pl.BlockSpec((BLOCK, qw), own_block),
        pl.BlockSpec((BLOCK, qw), oth_block),
        pl.BlockSpec((BLOCK, gw), own_block),
        pl.BlockSpec((BLOCK, gw), oth_block),
    ] + [piece] * 4
    arrays = list(window) + [query, q_oth, d_attn, g_oth] + list(weights)
    aliases = {}
    if not first:
        in_specs += [resident, resident, pl.BlockSpec(memory_space=pl.ANY)]
        arrays += list(carried)
        aliases = {len(arrays): 0}
    out_shapes = (
        [jax.ShapeDtypeStruct(query.shape, BF16), jax.ShapeDtypeStruct((BLOCK, HALF * qw), BF16)]
        + [jax.ShapeDtypeStruct((HALF, BAND, PAIR), BF16)] * 4
        + [
            jax.ShapeDtypeStruct((WINDOW, KV_RANK), F32),
            jax.ShapeDtypeStruct((WINDOW, ROPE), F32),
        ]
    )
    out_specs = (
        [pl.BlockSpec((BLOCK, qw), own_block), pl.BlockSpec((BLOCK, qw), lambda k, sc: (0, k))]
        + [piece] * 4
        + [
            pl.BlockSpec((WINDOW, KV_RANK), lambda k, sc: (0, 0)),
            pl.BlockSpec((WINDOW, ROPE), lambda k, sc: (0, 0)),
        ]
    )
    outs = pl.pallas_call(
        functools.partial(attend_kernel, color, first),
        out_shape=out_shapes,
        grid_spec=pltpu.PrefetchScalarGridSpec(
            num_scalar_prefetch=1,
            grid=(HALF,),
            in_specs=in_specs,
            out_specs=out_specs,
            scratch_shapes=[
                pltpu.VMEM((KV_RANK, PAIR), BF16),
                pltpu.VMEM((CHIP, qw), BF16),
                pltpu.VMEM((CHIP, gw), BF16),
                pltpu.VMEM((CHIP, qw), BF16),
                pltpu.VMEM((WINDOW, PAIR), BF16),
                pltpu.VMEM((KV_RANK, PAIR), BF16),
            ],
        ),
        input_output_aliases=aliases,
        cost_estimate=pl.CostEstimate(
            flops=HALF * 2 * 2 * WINDOW * (3 * KV_RANK * 256 + CHIP * (3 * QK + 2 * VDIM)),
            bytes_accessed=16 * 2**20,
            transcendentals=HALF * 2 * WINDOW * CHIP,
        ),
    )(scalars, *arrays)
    d_query, dq_oth = outs[:2]
    return dq_oth, outs[2:6], (outs[6], outs[7], d_query)


def place_kernel(sc, x0, x1, y0, y1, _, out):
    h = pl.program_id(0)
    width = 2 * QK
    for half, (xs, ys) in enumerate(((x0, y0), (x1, y1))):

        @pl.when(h == half)
        def _():
            out[:, :width] = xs[...]
            out[:, width:] = ys[...]


def place_received(core, received, d_query):
    width = 2 * QK
    low = pl.BlockSpec((BLOCK, width), lambda h, k, sc: (0, jnp.minimum(k + HALF * h, HALF - 1)))
    high = pl.BlockSpec((BLOCK, width), lambda h, k, sc: (0, jnp.maximum(k + HALF * h - HALF, 0)))
    return pl.pallas_call(
        place_kernel,
        out_shape=jax.ShapeDtypeStruct(d_query.shape, BF16),
        grid_spec=pltpu.PrefetchScalarGridSpec(
            num_scalar_prefetch=1,
            grid=(2, HALF),
            in_specs=[low, high, low, high, pl.BlockSpec(memory_space=pl.ANY)],
            out_specs=pl.BlockSpec(
                (BLOCK, 2 * width), lambda h, k, sc: (0, 2 * (k + HALF * h) + 1 - sc[0])
            ),
        ),
        input_output_aliases={5: 0},
        cost_estimate=pl.CostEstimate(
            flops=0, bytes_accessed=BLOCK * 16 * 2 * width, transcendentals=0
        ),
    )(core, *received, d_query)


def body(query, latent, d_attn, w_kv, doc_lengths):
    x, y, z, c = (lax.axis_index(name).astype(jnp.int32) for name in ("x", "y", "z", "core"))
    as_scalars = lambda *values: jnp.stack(values)
    s_core, s_x, s_y, s_z = (as_scalars(v) for v in (c, x, y, z))
    s_main = as_scalars(c, x, y)

    opposite = shift(w_kv, "z", HALF)
    couple = jnp.stack([w_kv, opposite])
    couples = [couple] + [shift(couple, "z", s) for s in Z_STEPS[1:]]
    by_z = z_assemble(s_z, couples)
    mid_axis, end_axis, mid_index = ("y", "x"), ("x", "y"), (s_y, s_x)
    mids = [shifts(by_z[color], mid_axis[color]) for color in range(2)]
    banded = [mid_assemble(mid_index[color], mids[color]) for color in range(2)]

    q_send, g_send = pack_other(s_core, query, d_attn)
    q_oth, g_oth = shift(q_send, "core", 1), shift(g_send, "core", 1)

    before = [shift(latent, "z", 2), shift(latent, "z", 1)]
    mine = jnp.stack(before + [latent])
    theirs = shift(mine, "core", 1)
    even = jnp.where(c == 0, mine, theirs)
    odd = jnp.where(c == 0, theirs, mine)
    reach = jnp.stack([even, odd], axis=1).reshape(6 * BLOCK, KV_RANK + ROPE)[BLOCK:]
    compressed = reach[:, :KV_RANK]

    ends = jnp.cumsum(doc_lengths[0])
    q_pos = z * CHIP + jnp.arange(CHIP, dtype=jnp.int32)
    k_pos = z * CHIP + (CHIP - WINDOW) + jnp.arange(WINDOW, dtype=jnp.int32)
    begin = jnp.max(jnp.where(ends[:, None] <= q_pos[None, :], ends[:, None], 0), axis=0)
    allowed = (k_pos[:, None] >= begin[None, :]) & (k_pos[:, None] <= q_pos[None, :])
    bias = jnp.where(allowed, 0.0, MASKED).astype(F32)
    window = (compressed, jnp.transpose(compressed), reach[:, KV_RANK:], bias)

    carried = None
    d_weights = {}
    received = {}
    gathered = {}
    for half in range(2):
        for color in range(2):
            gathered[color, half] = shifts(banded[color][half], end_axis[color])
    for half in range(2):
        for color in range(2):
            dq_oth, pieces, carried = attend(
                color, half, s_main, window, query, q_oth, d_attn, g_oth,
                gathered[color, half], carried,
            )
            received[color, half] = shift(dq_oth, "core", 1)
            d_weights[color, half] = scatter_shifts(pieces, end_axis[color])
    d_lat, d_rope, d_query = carried
    d_query = place_received(
        s_core, [received[0, 0], received[0, 1], received[1, 0], received[1, 1]], d_query
    )

    halves = []
    for color in range(2):
        summed = first_reduce(mid_index[color], d_weights[color, 0], d_weights[color, 1])
        halves.append(scatter_shifts(summed, mid_axis[color]))
    summed = second_reduce(s_z, halves[0], halves[1])
    couples = [summed[0]] + [shift(a, "z", s) for a, s in zip(summed[1:], Z_STEPS[1:])]
    near, far = third_reduce(s_z, couples)
    far = shift(far, "z", HALF)
    d_w_kv = near + far.astype(F32)

    terms = jnp.concatenate([d_lat, d_rope], axis=1)
    terms = jnp.pad(terms, ((BLOCK, 0), (0, 0))).reshape(3, NC, BLOCK, KV_RANK + ROPE)
    kept = jnp.where(c == 0, terms[:, 0], terms[:, 1])
    sent = jnp.where(c == 0, terms[:, 1], terms[:, 0]).astype(BF16)
    got = shift(sent, "core", 1)
    both = kept + got.astype(F32)
    back = both[:2].astype(BF16)
    one, two = shift(back[1], "z", -1), shift(back[0], "z", -2)
    d_latent = both[2] + one.astype(F32) + two.astype(F32)
    return d_query, d_latent, d_w_kv


def solution(mesh):
    split = Mesh(mesh.devices.reshape(NX, NY, NZ, NC), ("x", "y", "z", "core"))
    tokens = P(("x", "y", "z", "core"), None)
    weight = P(("x", "y"), ("z", "core"))
    return jax.shard_map(
        body,
        mesh=split,
        in_specs=(tokens, tokens, tokens, weight, P(("x", "y"), None)),
        out_specs=(tokens, tokens, weight),
        check_vma=False,
    )
```
